32 devices in a mesh: layer: 4 (over y, core), tok: 8 (over z, x).
Axes of the slice: x: 2, y: 2, z: 4, core: 2. Of those that a mesh axis runs over, the one named last changes fastest.
Arguments:
- inputs: bfloat16 [8, 5120, 4096], P('layer', 'tok'), may hold values from -6 to 6
- out_grads: bfloat16 [8, 5120, 4096], P('layer', 'tok'), may hold values from -6 to 6
- a_inverse: bfloat16 [8, 4096, 4096], P('layer', None, 'tok'), as said below
- g_inverse: bfloat16 [8, 4096, 4096], P('layer', None, 'tok'), as said below
- query_in: bfloat16 [8, 8, 8, 4096], P('layer', None, None, 'tok'), may hold values from -0.03125 to 0.03125
- query_out: bfloat16 [8, 8, 8, 4096], P('layer', None, None, 'tok'), may hold values from -0.03125 to 0.03125
Outputs:
- scores: float32 [5120, 8], P('tok', 'layer')
The draws below stay inside these ranges and needn't reach their ends.
Inputs may be any that keep to these rules, and one draw needn't show every extreme that they name: `a_inverse`: each layer's factor is the identity plus independent entries of deviation D ** -0.5. `g_inverse`: each layer's factor is the identity plus independent entries of deviation D ** -0.5.
All inputs are finite; a program needn't handle non-finite values.
Results may differ from the reference program's by a relative error of at most 0.0041.
Values may be sent and summed in bfloat16 or wider, within the bound.
No kernel may reach another device: no remote copies, remote signals or barrier semaphores. Data moves between devices by JAX's collectives and lax.ppermute only.
A program may use at most 128 MiB of HBM per device.

```python
import jax
import jax.numpy as jnp

D = 4096
RANK = 8
LAYERS = 8
TOKENS = 5120
QUERIES = 8


def factor_draw(key, salt):
    noise = jax.random.normal(jax.random.fold_in(key, salt), (LAYERS, D, D), jnp.float32) * D ** (-0.5)
    return (noise + jnp.eye(D, dtype=jnp.float32)[None]).astype(jnp.bfloat16)


def draw_a_inverse(key, part):
    return factor_draw(key, 11)


def draw_g_inverse(key, part):
    return factor_draw(key, 23)


def steps_of(stream_key, extent, shards, smallest, largest):
    factor_of, own = 1.0, jax.random.fold_in(stream_key, 6)
    for position, shards_of in shards:
        heights = jnp.exp(jax.random.uniform(jax.random.fold_in(own, position), (shards_of,), jnp.float32, smallest / len(shards), largest / len(shards)))
        factor_of = factor_of * jnp.repeat(heights, extent[position] // shards_of).reshape([-1 if axis == position else 1 for axis in range(len(extent))])
    return factor_of


def scatter_about(rng, shape, deviation, bound, shards=(), kind=jnp.bfloat16):
    loudness = steps_of(rng, shape, shards, -0.22, 0.18) if shards else 1.0
    drawn = jax.random.normal(rng, shape, jnp.float32) * deviation * loudness
    return jnp.minimum(jnp.maximum(drawn, -bound), bound).astype(kind)


def setup_inputs(seed: int = 0) -> dict:
    seeds = jax.random.split(jax.random.key(seed), 7)
    inputs = scatter_about(seeds[0], (LAYERS, TOKENS, D), 1.0, 6.0, ((0, 4), (1, 8)))
    out_grads = scatter_about(seeds[1], (LAYERS, TOKENS, D), 1.0, 6.0, ((0, 4), (1, 8)))
    a_inverse = draw_a_inverse(jax.random.fold_in(seeds[6], 71), 0)
    g_inverse = draw_g_inverse(jax.random.fold_in(seeds[6], 71), 0)
    query_in = scatter_about(seeds[4], (LAYERS, QUERIES, RANK, D), (8 * D) ** -0.5, 0.03125, ((0, 4), (3, 8)))
    query_out = scatter_about(seeds[5], (LAYERS, QUERIES, RANK, D), (8 * D) ** -0.5, 0.03125, ((0, 4), (3, 8)))
    return {"inputs": inputs, "out_grads": out_grads, "a_inverse": a_inverse, "g_inverse": g_inverse, "query_in": query_in, "query_out": query_out}


def reference(inputs, out_grads, a_inverse, g_inverse, query_in, query_out):
    scores = jnp.zeros((inputs.shape[1], query_in.shape[1]), jnp.float32)
    for layer_no in range(inputs.shape[0]):
        pre_in = jnp.einsum("qrj,ij->qri", query_in[layer_no], a_inverse[layer_no], preferred_element_type=jnp.float32).astype(jnp.bfloat16)
        pre_out = jnp.einsum("qrj,ij->qri", query_out[layer_no], g_inverse[layer_no], preferred_element_type=jnp.float32).astype(jnp.bfloat16)
        side_in = jnp.einsum("td,qrd->tqr", inputs[layer_no], pre_in, preferred_element_type=jnp.float32)
        side_out = jnp.einsum("td,qrd->tqr", out_grads[layer_no], pre_out, preferred_element_type=jnp.float32)
        scores = scores + jnp.sum(side_in * side_out, axis=2)
    return scores
```

```python
import functools

import jax
import jax.numpy as jnp
from jax import lax
from jax.experimental import pallas as pl
from jax.experimental.pallas import tpu as pltpu
from jax.sharding import PartitionSpec as P

NT = (((1,), (1,)), ((), ()))
NN = (((1,), (0,)), ((), ()))


def halving_order(bits):
    kept = [0]
    for bit in reversed(bits[1:]):
        kept = [p | bit for p in kept] + kept
    return kept


def precondition_kernel(chunk_ref, q_ref, a_ref, sent_ref, kept_ref, w_ref):
    step = pl.program_id(0)
    half = pl.num_programs(0) // 2
    layers, vectors, _ = q_ref.shape

    @pl.when(step == 0)
    def _():
        w_ref[...] = jnp.zeros_like(w_ref)
        for k in range(layers):
            w_ref[k, k * vectors : (k + 1) * vectors, :] = q_ref[k]

    total = lax.dot_general(a_ref[0], w_ref[0], NT, preferred_element_type=jnp.float32)
    for k in range(1, layers):
        total += lax.dot_general(a_ref[k], w_ref[k], NT, preferred_element_type=jnp.float32)

    @pl.when(step < half)
    def _():
        sent_ref[0] = total.astype(sent_ref.dtype)

    @pl.when(step >= half)
    def _():
        kept_ref[0] = total


def precondition(query, inverse, chunks, shards):
    layers, width, depth = inverse.shape
    vectors = query.shape[1]
    lanes = layers * vectors
    rows = width // shards
    half = shards // 2
    return pl.pallas_call(
        precondition_kernel,
        grid_spec=pltpu.PrefetchScalarGridSpec(
            num_scalar_prefetch=1,
            grid=(shards,),
            in_specs=[
                pl.BlockSpec(query.shape, lambda t, c: (0, 0, 0)),
                pl.BlockSpec((layers, rows, depth), lambda t, c: (0, c[t], 0)),
            ],
            out_specs=[
                pl.BlockSpec((1, rows, lanes), lambda t, c: (jnp.minimum(t, half - 1), 0, 0)),
                pl.BlockSpec((1, rows, lanes), lambda t, c: (jnp.maximum(t - half, 0), 0, 0)),
            ],
            scratch_shapes=[pltpu.VMEM((layers, lanes, depth), query.dtype)],
        ),
        out_shape=[
            jax.ShapeDtypeStruct((half, rows, lanes), jnp.bfloat16),
            jax.ShapeDtypeStruct((half, rows, lanes), jnp.float32),
        ],
        name="precondition",
    )(chunks, query, inverse)


def score_kernel(shares, queries, *refs):
    n = len(shares)
    x_ref, g_ref = refs[2], refs[3]
    in_refs, out_refs = refs[4 : 4 + n], refs[4 + n : 4 + 2 * n]
    o_ref, acc_ref = refs[4 + 2 * n], refs[5 + 2 * n]
    step = pl.program_id(0)
    layers = x_ref.shape[0]
    lanes = acc_ref.shape[-1]
    per_layer = lanes // layers

    def chosen(pieces):
        value, end = pieces[0][0], shares[0]
        for piece, share in zip(pieces[1:], shares[1:]):
            value = jnp.where(step >= end, piece[0], value)
            end += share
        return value

    @pl.when(step == 0)
    def _():
        acc_ref[...] = jnp.zeros_like(acc_ref)

    for side, (tokens, pieces) in enumerate(((x_ref, in_refs), (g_ref, out_refs))):
        weights = chosen(pieces)
        for k in range(layers):
            acc_ref[side, k] += lax.dot_general(
                tokens[k], weights, NN, preferred_element_type=jnp.float32
            )

    @pl.when(step == pl.num_programs(0) - 1)
    def _():
        lane = lax.broadcasted_iota(jnp.int32, (acc_ref.shape[2], lanes), 1)
        product = acc_ref[0, 0] * acc_ref[1, 0]
        for k in range(1, layers):
            product = jnp.where(
                lane >= k * per_layer, acc_ref[0, k] * acc_ref[1, k], product
            )
        rank = per_layer // queries
        row = lax.broadcasted_iota(jnp.int32, (queries, lanes), 0)
        column = lax.broadcasted_iota(jnp.int32, (queries, lanes), 1)
        select = ((column % per_layer) // rank == row).astype(jnp.float32)
        o_ref[...] = lax.dot_general(
            select, product, NT, precision=lax.Precision.HIGHEST,
            preferred_element_type=jnp.float32,
        )


def scores(inputs, out_grads, pre_in, pre_out, chunks_in, chunks_out, queries, shards):
    layers, tokens, width = inputs.shape
    _, rows, lanes = pre_in[0].shape
    shares = [piece.shape[0] for piece in pre_in]
    token_block = (layers, tokens, rows)
    specs, end = [], 0
    for share in shares:
        specs.append(
            pl.BlockSpec(
                (1, rows, lanes),
                functools.partial(
                    lambda s, n, t, a, b: (jnp.clip(t - s, 0, n - 1), 0, 0), end, share
                ),
            )
        )
        end += share
    return pl.pallas_call(
        functools.partial(score_kernel, shares, queries),
        grid_spec=pltpu.PrefetchScalarGridSpec(
            num_scalar_prefetch=2,
            grid=(shards,),
            in_specs=[
                pl.BlockSpec(token_block, lambda t, a, b: (0, 0, a[t])),
                pl.BlockSpec(token_block, lambda t, a, b: (0, 0, b[t])),
            ]
            + specs
            + specs,
            out_specs=pl.BlockSpec((queries, tokens), lambda t, a, b: (0, 0)),
            scratch_shapes=[pltpu.VMEM((2, layers, tokens, lanes), jnp.float32)],
        ),
        out_shape=jax.ShapeDtypeStruct((queries, tokens), jnp.float32),
        name="scores",
    )(chunks_in, chunks_out, inputs, out_grads, *pre_in, *pre_out)


def swap(value, axis, size, bit):
    return lax.ppermute(value, axis, [(i, i ^ bit) for i in range(size)])


def reduce_and_gather(sent, kept, bits, shards):
    for bit in bits[:-1]:
        kept = kept + swap(sent, "tok", shards, bit).astype(jnp.float32)
        half = kept.shape[0] // 2
        sent, kept = kept[:half].astype(jnp.bfloat16), kept[half:]
    own = (kept + swap(sent, "tok", shards, bits[-1]).astype(jnp.float32)).astype(jnp.bfloat16)
    pieces = [own]
    for bit in reversed(bits):
        here = pieces[0] if len(pieces) == 1 else jnp.concatenate(pieces, axis=0)
        pieces = [swap(here, "tok", shards, bit)] + pieces
    return pieces


def local(shards, layer_devices, inputs, out_grads, a_inverse, g_inverse, query_in, query_out):
    layers, queries, rank, depth = query_in.shape
    me = lax.axis_index("tok")
    bits = [1 << b for b in range(shards.bit_length() - 1)]
    bits_in, bits_out = bits, [bits[1], bits[0]] + bits[2:]

    def order(bits):
        kept = halving_order(bits)
        return jnp.array([p | bits[0] for p in kept] + kept, jnp.int32) ^ me

    chunks_in, chunks_out = order(bits_in), order(bits_out)
    flat = (layers, queries * rank, depth)
    sent_in, kept_in = precondition(query_in.reshape(flat), a_inverse, chunks_in, shards)
    sent_out, kept_out = precondition(query_out.reshape(flat), g_inverse, chunks_out, shards)
    pre_in = reduce_and_gather(sent_in, kept_in, bits_in, shards)
    pre_out = reduce_and_gather(sent_out, kept_out, bits_out, shards)
    partial = scores(
        inputs, out_grads, pre_in, pre_out, chunks_in, chunks_out, queries, shards
    )
    share = queries // layer_devices
    blocks = partial.reshape(layer_devices, share, partial.shape[1])
    here = lax.axis_index("layer")
    total = lax.dynamic_index_in_dim(blocks, here, 0, keepdims=False)
    for other in range(1, layer_devices):
        away = lax.dynamic_index_in_dim(blocks, here ^ other, 0, keepdims=False)
        total = total + swap(away, "layer", layer_devices, other)
    return total.T


def solution(mesh):
    in_specs = (
        P("layer", "tok", None),
        P("layer", "tok", None),
        P("layer", None, "tok"),
        P("layer", None, "tok"),
        P("layer", None, None, "tok"),
        P("layer", None, None, "tok"),
    )
    out_specs = P("tok", "layer")
    body = functools.partial(local, mesh.shape["tok"], mesh.shape["layer"])
    return jax.shard_map(body, mesh=mesh, in_specs=in_specs, out_specs=out_specs, check_vma=False)
```

```python
import functools

import jax
import jax.numpy as jnp
from jax import lax
from jax.experimental import pallas as pl
from jax.experimental.pallas import tpu as pltpu
from jax.sharding import PartitionSpec as P

NT = (((1,), (1,)), ((), ()))
NN = (((1,), (0,)), ((), ()))
MIB = 1 << 20


def kept_positions(bits):
    kept = [0]
    for bit in reversed(bits[1:]):
        kept = [p | bit for p in kept] + kept
    return kept


def precondition_kernel(positions, q_hbm, a_hbm, first_ref, second_ref, a_vmem, w_ref, sems, q_sems):
    layers, vectors, _ = q_hbm.shape
    rows = first_ref.shape[1]
    me = lax.axis_index("tok")
    copies, q_copies = [], []
    for k in range(layers):
        here = pl.ds(k * vectors, vectors)
        q_copies.append(pltpu.make_async_copy(q_hbm.at[k], w_ref.at[k, here, :], q_sems.at[k]))
        q_copies[-1].start()
    for i, p in enumerate(positions):
        begin = pl.multiple_of((me ^ p) * rows, rows)
        copy = pltpu.make_async_copy(
            a_hbm.at[:, pl.ds(begin, rows), :], a_vmem.at[i], sems.at[i]
        )
        copy.start()
        copies.append(copy)
    for k in range(layers):
        for other in range(layers):
            if other != k:
                w_ref[k, other * vectors : (other + 1) * vectors, :] = jnp.zeros(
                    (vectors, w_ref.shape[2]), w_ref.dtype
                )
    for copy in q_copies:
        copy.wait()
    half = first_ref.shape[0]
    for i, copy in enumerate(copies):
        copy.wait()
        total = lax.dot_general(a_vmem[i, 0], w_ref[0], NT, preferred_element_type=jnp.float32)
        for k in range(1, layers):
            total += lax.dot_general(
                a_vmem[i, k], w_ref[k], NT, preferred_element_type=jnp.float32
            )
        target = first_ref if i < half else second_ref
        target[i % half] = total.astype(target.dtype)


def precondition(query, inverse, positions, rows, dtype, name):
    layers, vectors, depth = query.shape
    lanes = layers * vectors
    count = len(positions)
    return pl.pallas_call(
        functools.partial(precondition_kernel, positions),
        in_specs=[pl.BlockSpec(memory_space=pl.ANY)] * 2,
        out_specs=[pl.BlockSpec(memory_space=pltpu.VMEM)] * 2,
        out_shape=[jax.ShapeDtypeStruct((count // 2, rows, lanes), dtype)] * 2,
        scratch_shapes=[
            pltpu.VMEM((count, layers, rows, depth), inverse.dtype),
            pltpu.VMEM((layers, lanes, depth), query.dtype),
            pltpu.SemaphoreType.DMA((count,)),
            pltpu.SemaphoreType.DMA((layers,)),
        ],
        compiler_params=pltpu.CompilerParams(vmem_limit_bytes=20 * MIB),
        name=name,
    )(query, inverse)


def add_products(tokens_ref, pieces, acc_ref, rows, side=None):
    me = lax.axis_index("tok")
    for k in range(tokens_ref.shape[0]):
        total = None
        for p, ref, i in pieces:
            begin = pl.multiple_of((me ^ p) * rows, rows)
            product = lax.dot_general(
                tokens_ref[k, :, pl.ds(begin, rows)], ref[i], NN,
                preferred_element_type=jnp.float32,
            )
            total = product if total is None else total + product
        yield k, total


def spread(pieces, refs):
    return [(p, ref, i) for (ps, _), ref in zip(pieces, refs) for i, p in enumerate(ps)]


def partial_kernel(pieces, first, *refs):
    n = len(pieces)
    tokens_ref, weights = refs[0], refs[1 : 1 + n]
    acc_in = None if first else refs[1 + n]
    acc_ref = refs[-1]
    rows = weights[0].shape[1]
    for k, total in add_products(tokens_ref, spread(pieces, weights), acc_ref, rows):
        acc_ref[k] = total if first else acc_in[k] + total


def partial_scores(tokens, pieces, acc, name):
    layers, count, _ = tokens.shape
    lanes = pieces[0][1].shape[2]
    arrays = [a for _, a in pieces]
    operands = [tokens] + arrays + ([] if acc is None else [acc])
    return pl.pallas_call(
        functools.partial(partial_kernel, pieces, acc is None),
        in_specs=[pl.BlockSpec(memory_space=pltpu.VMEM)] * len(operands),
        out_specs=pl.BlockSpec(memory_space=pltpu.VMEM),
        out_shape=jax.ShapeDtypeStruct((layers, count, lanes), jnp.float32),
        input_output_aliases={} if acc is None else {len(operands) - 1: 0},
        compiler_params=pltpu.CompilerParams(vmem_limit_bytes=8 * MIB),
        name=name,
    )(*operands)


def last_kernel(pieces_in, pieces_out, queries, layer_devices, *refs):
    x_ref, g_ref, acc_x, acc_g = refs[:4]
    weights_in = refs[4 : 4 + len(pieces_in)]
    weights_out = refs[4 + len(pieces_in) : 4 + len(pieces_in) + len(pieces_out)]
    outs = refs[4 + len(pieces_in) + len(pieces_out) :]
    rows, lanes = weights_in[0].shape[1:]
    layers, count, _ = acc_x.shape
    per_layer = lanes // layers
    rank = per_layer // queries
    lane = lax.broadcasted_iota(jnp.int32, (count, lanes), 1)
    product = None
    for (k, x), (_, g) in zip(
        add_products(x_ref, spread(pieces_in, weights_in), acc_x, rows),
        add_products(g_ref, spread(pieces_out, weights_out), acc_g, rows),
    ):
        here = (acc_x[k] + x) * (acc_g[k] + g)
        product = here if product is None else jnp.where(lane >= k * per_layer, here, product)
    share = queries // layer_devices
    row = lax.broadcasted_iota(jnp.int32, (queries, lanes), 0)
    column = lax.broadcasted_iota(jnp.int32, (queries, lanes), 1)
    query = ((row // share) ^ lax.axis_index("layer")) * share + row % share
    select = ((column % per_layer) // rank == query).astype(jnp.float32)
    summed = lax.dot_general(
        select, product, NT, precision=lax.Precision.HIGHEST, preferred_element_type=jnp.float32
    )
    for i, out in enumerate(outs):
        out[...] = summed[i * share : (i + 1) * share, :]


def last_scores(inputs, out_grads, acc_x, acc_g, pieces_in, pieces_out, queries, layer_devices):
    operands = [inputs, out_grads, acc_x, acc_g]
    operands += [a for _, a in pieces_in] + [a for _, a in pieces_out]
    share = queries // layer_devices
    return pl.pallas_call(
        functools.partial(last_kernel, pieces_in, pieces_out, queries, layer_devices),
        in_specs=[pl.BlockSpec(memory_space=pltpu.VMEM)] * len(operands),
        out_specs=[pl.BlockSpec(memory_space=pltpu.VMEM)] * layer_devices,
        out_shape=[jax.ShapeDtypeStruct((share, inputs.shape[1]), jnp.float32)] * layer_devices,
        compiler_params=pltpu.CompilerParams(vmem_limit_bytes=12 * MIB),
        name="last_scores",
    )(*operands)


def swap(value, axis, size, bit):
    return lax.ppermute(value, axis, [(i, i ^ bit) for i in range(size)])


def reduce_to_owner(sent, kept, bits, shards):
    for bit in bits[:-1]:
        first = kept[0] + swap(sent[0], "tok", shards, bit).astype(jnp.float32)
        second = kept[1] + swap(sent[1], "tok", shards, bit).astype(jnp.float32)
        half = first.shape[0] // 2
        if half == 0:
            break
        first = first.astype(jnp.bfloat16)
        sent, kept = (first[:half], first[half:]), (second[:half], second[half:])
    first = first.astype(jnp.bfloat16)
    return (second + swap(first, "tok", shards, bits[-1]).astype(jnp.float32)).astype(jnp.bfloat16)


def gather_chunks(own, bits, shards):
    held, arrived = [((0,), own)], []
    for bit in reversed(bits):
        arrived = [
            (tuple(p | bit for p in ps), swap(a, "tok", shards, bit)) for ps, a in held
        ]
        if bit == bits[0]:
            break
        if len(arrived) > 1:
            joined = jnp.concatenate([a for _, a in arrived], axis=0)
            arrived = [(tuple(p for ps, _ in arrived for p in ps), joined)]
        held = held + arrived
    return held, arrived


def local(shards, layer_devices, inputs, out_grads, a_inverse, g_inverse, query_in, query_out):
    layers, queries, rank, depth = query_in.shape
    rows = a_inverse.shape[1] // shards
    bits = [1 << b for b in range(shards.bit_length() - 1)]
    sides = (
        ("in", query_in, a_inverse, bits, inputs),
        ("out", query_out, g_inverse, [bits[1], bits[0]] + bits[2:], out_grads),
    )
    flat = (layers, queries * rank, depth)
    accs, lasts = [], []
    for name, query, inverse, order, tokens in sides:
        kept_at = kept_positions(order)
        query = query.reshape(flat)
        sent = precondition(
            query, inverse, [p | order[0] for p in kept_at], rows, jnp.bfloat16, "sent_" + name
        )
        kept = precondition(query, inverse, kept_at, rows, jnp.float32, "kept_" + name)
        own = reduce_to_owner(sent, kept, order, shards)
        early, late = gather_chunks(own, order, shards)
        acc = partial_scores(tokens, early, None, "early_" + name)
        accs.append(partial_scores(tokens, late[:-1], acc, "middle_" + name))
        lasts.append(late[-1:])
    shares = last_scores(
        inputs, out_grads, accs[0], accs[1], lasts[0], lasts[1], queries, layer_devices
    )
    total = shares[0]
    for other in range(1, layer_devices):
        total = total + swap(shares[other], "layer", layer_devices, other)
    return total.T


def solution(mesh):
    in_specs = (
        P("layer", "tok", None),
        P("layer", "tok", None),
        P("layer", None, "tok"),
        P("layer", None, "tok"),
        P("layer", None, None, "tok"),
        P("layer", None, None, "tok"),
    )
    out_specs = P("tok", "layer")
    body = functools.partial(local, mesh.shape["tok"], mesh.shape["layer"])
    return jax.shard_map(body, mesh=mesh, in_specs=in_specs, out_specs=out_specs, check_vma=False)
```

```python
import functools

import jax
import jax.numpy as jnp
from jax import lax
from jax.experimental import pallas as pl
from jax.experimental.pallas import tpu as pltpu
from jax.sharding import PartitionSpec as P

NT = (((1,), (1,)), ((), ()))
MIB = 1 << 20


def kept_positions(bits):
    kept = [0]
    for bit in reversed(bits[1:]):
        kept = [p | bit for p in kept] + kept
    return kept


def precondition_kernel(positions, q_hbm, a_hbm, first_ref, second_ref, q_vmem, a_vmem, sems, q_sem):
    layers, vectors, _ = q_hbm.shape
    rows = first_ref.shape[2]
    me = lax.axis_index("tok")
    q_copy = pltpu.make_async_copy(q_hbm, q_vmem, q_sem)
    q_copy.start()
    copies = []
    for i, p in enumerate(positions):
        begin = pl.multiple_of((me ^ p) * rows, rows)
        copies.append(
            pltpu.make_async_copy(a_hbm.at[:, pl.ds(begin, rows), :], a_vmem.at[i], sems.at[i])
        )
        copies[-1].start()
    q_copy.wait()
    half = first_ref.shape[0]
    for i, copy in enumerate(copies):
        copy.wait()
        target = first_ref if i < half else second_ref
        for k in range(layers):
            product = lax.dot_general(
                q_vmem[k], a_vmem[i, k], NT, preferred_element_type=jnp.float32
            )
            target[i % half, k * vectors : (k + 1) * vectors, :] = product.astype(target.dtype)


def precondition(query, inverse, positions, rows, dtype, name):
    layers, vectors, depth = query.shape
    lanes = layers * vectors
    count = len(positions)
    return pl.pallas_call(
        functools.partial(precondition_kernel, positions),
        in_specs=[pl.BlockSpec(memory_space=pltpu.HBM)] * 2,
        out_specs=[pl.BlockSpec(memory_space=pltpu.VMEM)] * 2,
        out_shape=[jax.ShapeDtypeStruct((count // 2, lanes, rows), dtype)] * 2,
        scratch_shapes=[
            pltpu.VMEM(query.shape, query.dtype),
            pltpu.VMEM((count, layers, rows, depth), inverse.dtype),
            pltpu.SemaphoreType.DMA((count,)),
            pltpu.SemaphoreType.DMA(()),
        ],
        compiler_params=pltpu.CompilerParams(vmem_limit_bytes=16 * MIB),
        name=name,
    )(
        pltpu.with_memory_space_constraint(query, pltpu.HBM),
        pltpu.with_memory_space_constraint(inverse, pltpu.HBM),
    )


def add_products(tokens_ref, pieces, rows):
    me = lax.axis_index("tok")
    for k in range(tokens_ref.shape[0]):
        total = None
        for p, ref, i in pieces:
            begin = pl.multiple_of((me ^ p) * rows, rows)
            product = lax.dot_general(
                tokens_ref[k, :, pl.ds(begin, rows)], ref[i], NT,
                preferred_element_type=jnp.float32,
            )
            total = product if total is None else total + product
        yield k, total


def spread(pieces, refs):
    return [(p, ref, i) for (ps, _), ref in zip(pieces, refs) for i, p in enumerate(ps)]


def partial_kernel(pieces, first, *refs):
    n = len(pieces)
    tokens_ref, weights = refs[0], refs[1 : 1 + n]
    acc_in = None if first else refs[1 + n]
    acc_ref = refs[-1]
    rows = weights[0].shape[2]
    for k, total in add_products(tokens_ref, spread(pieces, weights), rows):
        acc_ref[k] = total if first else acc_in[k] + total


def partial_scores(tokens, pieces, acc, name):
    layers, count, _ = tokens.shape
    lanes = pieces[0][1].shape[1]
    arrays = [a for _, a in pieces]
    operands = [tokens] + arrays + ([] if acc is None else [acc])
    return pl.pallas_call(
        functools.partial(partial_kernel, pieces, acc is None),
        in_specs=[pl.BlockSpec(memory_space=pltpu.VMEM)] * len(operands),
        out_specs=pl.BlockSpec(memory_space=pltpu.VMEM),
        out_shape=jax.ShapeDtypeStruct((layers, count, lanes), jnp.float32),
        input_output_aliases={} if acc is None else {len(operands) - 1: 0},
        compiler_params=pltpu.CompilerParams(vmem_limit_bytes=8 * MIB),
        name=name,
    )(*operands)


def last_kernel(pieces_in, pieces_out, queries, layer_devices, *refs):
    x_ref, g_ref, acc_x, acc_g = refs[:4]
    weights_in = refs[4 : 4 + len(pieces_in)]
    weights_out = refs[4 + len(pieces_in) : 4 + len(pieces_in) + len(pieces_out)]
    outs = refs[4 + len(pieces_in) + len(pieces_out) :]
    lanes, rows = weights_in[0].shape[1:]
    layers, count, _ = acc_x.shape
    per_layer = lanes // layers
    rank = per_layer // queries
    lane = lax.broadcasted_iota(jnp.int32, (count, lanes), 1)
    product = None
    for (k, x), (_, g) in zip(
        add_products(x_ref, spread(pieces_in, weights_in), rows),
        add_products(g_ref, spread(pieces_out, weights_out), rows),
    ):
        here = (acc_x[k] + x) * (acc_g[k] + g)
        product = here if product is None else jnp.where(lane >= k * per_layer, here, product)
    share = queries // layer_devices
    row = lax.broadcasted_iota(jnp.int32, (queries, lanes), 0)
    column = lax.broadcasted_iota(jnp.int32, (queries, lanes), 1)
    query = ((row // share) ^ lax.axis_index("layer")) * share + row % share
    select = ((column % per_layer) // rank == query).astype(jnp.float32)
    summed = lax.dot_general(
        select, product, NT, precision=lax.Precision.HIGHEST, preferred_element_type=jnp.float32
    )
    for i, out in enumerate(outs):
        out[...] = summed[i * share : (i + 1) * share, :]


def last_scores(inputs, out_grads, acc_x, acc_g, pieces_in, pieces_out, queries, layer_devices):
    operands = [inputs, out_grads, acc_x, acc_g]
    operands += [a for _, a in pieces_in] + [a for _, a in pieces_out]
    share = queries // layer_devices
    return pl.pallas_call(
        functools.partial(last_kernel, pieces_in, pieces_out, queries, layer_devices),
        in_specs=[pl.BlockSpec(memory_space=pltpu.VMEM)] * len(operands),
        out_specs=[pl.BlockSpec(memory_space=pltpu.VMEM)] * layer_devices,
        out_shape=[jax.ShapeDtypeStruct((share, inputs.shape[1]), jnp.float32)] * layer_devices,
        compiler_params=pltpu.CompilerParams(vmem_limit_bytes=12 * MIB),
        name="last_scores",
    )(*operands)


def swap(value, axis, size, bit):
    return lax.ppermute(value, axis, [(i, i ^ bit) for i in range(size)])


def reduce_to_owner(sent, kept, bits, shards):
    for bit in bits[:-1]:
        first = kept[0] + swap(sent[0], "tok", shards, bit).astype(jnp.float32)
        second = kept[1] + swap(sent[1], "tok", shards, bit).astype(jnp.float32)
        half = first.shape[0] // 2
        if half == 0:
            break
        first = first.astype(jnp.bfloat16)
        sent, kept = (first[:half], first[half:]), (second[:half], second[half:])
    first = first.astype(jnp.bfloat16)
    return (second + swap(first, "tok", shards, bits[-1]).astype(jnp.float32)).astype(jnp.bfloat16)


def gather_chunks(own, bits, shards):
    held, arrived = [((0,), own)], []
    for bit in reversed(bits):
        arrived = [
            (tuple(p | bit for p in ps), swap(a, "tok", shards, bit)) for ps, a in held
        ]
        if bit == bits[0]:
            break
        if len(arrived) > 1:
            joined = jnp.concatenate([a for _, a in arrived], axis=0)
            arrived = [(tuple(p for ps, _ in arrived for p in ps), joined)]
        held = held + arrived
    return held, arrived


def local(shards, layer_devices, inputs, out_grads, a_inverse, g_inverse, query_in, query_out):
    layers, queries, rank, depth = query_in.shape
    rows = a_inverse.shape[1] // shards
    bits = [1 << b for b in range(shards.bit_length() - 1)]
    sides = (
        ("in", query_in, a_inverse, bits, inputs),
        ("out", query_out, g_inverse, [bits[1], bits[0]] + bits[2:], out_grads),
    )
    flat = (layers, queries * rank, depth)
    accs, lasts = [], []
    for name, query, inverse, order, tokens in sides:
        kept_at = kept_positions(order)
        query = query.reshape(flat)
        sent = precondition(
            query, inverse, [p | order[0] for p in kept_at], rows, jnp.bfloat16, "sent_" + name
        )
        kept = precondition(query, inverse, kept_at, rows, jnp.float32, "kept_" + name)
        own = reduce_to_owner(sent, kept, order, shards)
        early, late = gather_chunks(own, order, shards)
        acc = partial_scores(tokens, early, None, "early_" + name)
        accs.append(partial_scores(tokens, late[:-1], acc, "middle_" + name))
        lasts.append(late[-1:])
    shares = last_scores(
        inputs, out_grads, accs[0], accs[1], lasts[0], lasts[1], queries, layer_devices
    )
    total = shares[0]
    for other in range(1, layer_devices):
        total = total + swap(shares[other], "layer", layer_devices, other)
    return total.T


def solution(mesh):
    in_specs = (
        P("layer", "tok", None),
        P("layer", "tok", None),
        P("layer", None, "tok"),
        P("layer", None, "tok"),
        P("layer", None, None, "tok"),
        P("layer", None, None, "tok"),
    )
    out_specs = P("tok", "layer")
    body = functools.partial(local, mesh.shape["tok"], mesh.shape["layer"])
    return jax.shard_map(body, mesh=mesh, in_specs=in_specs, out_specs=out_specs, check_vma=False)
```
